32 devices in a mesh: lat: 8 (over z, x), lon: 4 (over y, core).
Axes of the slice: x: 2, y: 2, z: 4, core: 2. Of those that a mesh axis runs over, the one named last changes fastest.
Arguments:
- sky_map: bfloat16 [256, 8, 8192], P('lat', None, 'lon'), may hold values from -6 to 6
- legendre: bfloat16 [256, 2048, 512], P('lat', None, 'lon'), may hold values from -0.5 to 0.5
- conv_weight: bfloat16 [9, 8, 8], replicated, may hold values from -0.75 to 0.75
- block_ids: int32 [4], replicated, may hold values from 0 to 15, as said below
Outputs:
- harmonics: float32 [2048, 16, 512], P('lat', None, 'lon')
- local_conv: bfloat16 [256, 8, 8192], P('lat', None, 'lon')
The draws below stay inside these ranges and needn't reach their ends.
Inputs may be any that keep to these rules, and one draw needn't show every extreme that they name: `block_ids`: distinct m-block numbers in increasing order; the first is 0 and the last is 15.
All inputs are finite; a program needn't handle non-finite values.
Results may differ from the reference program's by a relative error of at most 0.0049.
Values may be sent and summed in bfloat16 or wider, within the bound.
A program may use at most 128 MiB of HBM per device.

```python
import jax
import jax.numpy as jnp
from jax import lax

C = 8
NPHI = 8192
L = 2048
MBLK = 128
KW = 4
R_DEV = 32
CYCLES = 256
NBLK = 4
M = 512
N_LAT = 8


def draw_block_ids(key, part):
    highest = L // MBLK - 1
    middle = jax.random.permutation(key, highest - 1)[:NBLK - 2] + 1
    middle = jnp.sort(middle).astype(jnp.int32)
    return jnp.concatenate([jnp.zeros((1,), jnp.int32), middle, jnp.full((1,), highest, jnp.int32)])


def strengthened(entries, key, source, target, shards_of, factor):
    owner, partner = [(jnp.arange(entries.shape[dim]) // (entries.shape[dim] // shards_of)).reshape([-1 if axis == dim else 1 for axis in range(entries.ndim)]) for dim in (source, target)]
    chosen = jax.random.permutation(key, shards_of)[partner]
    strong = (owner == chosen) | (owner == (partner + shards_of // 2) % shards_of)
    return jnp.where(strong, factor * entries, entries)


def shard_levels(stream_key, dims, pieces, low, largest):
    gain = 1.0
    for position, parts in pieces:
        steps = jax.random.uniform(jax.random.fold_in(jax.random.fold_in(stream_key, 6), position), (parts,), jnp.float32, low / len(pieces), largest / len(pieces))
        gain = gain * jnp.repeat(jnp.exp(steps), dims[position] // parts).reshape((-1,) + (1,) * (len(dims) - 1 - position))
    return gain


def normal_values(key, extent, width, reach, pieces=(), kind=jnp.bfloat16):
    array = width * jax.random.normal(key, extent, jnp.float32)
    if pieces:
        array = array * shard_levels(key, extent, pieces, -0.22, 0.18)
    return jnp.clip(array, -reach, reach).astype(kind)


def gaussian_with(stream_key, shape, deviation, limit, pieces, heavy, kind=jnp.bfloat16):
    array = deviation * jax.random.normal(stream_key, shape, jnp.float32)
    if pieces:
        array = array * shard_levels(stream_key, shape, pieces, -0.22, 0.18)
    return jnp.clip(strengthened(array, jax.random.fold_in(stream_key, 3), *heavy), -limit, limit).astype(kind)


def setup_inputs(seed: int = 0) -> dict:
    key_of = jax.random.split(jax.random.key(seed), 5)
    return {
        "sky_map": normal_values(key_of[0], (CYCLES, C, NPHI), 1.0, 6.0, ((0, 8), (2, 4))),
        "legendre": gaussian_with(key_of[1], (CYCLES, L, M), CYCLES ** -0.5, 0.5, ((0, 8), (2, 4)), (0, 1, 8, 2.0)),
        "conv_weight": normal_values(key_of[2], (2 * KW + 1, C, C), ((2 * KW + 1) * C) ** -0.5, 0.75),
        "block_ids": draw_block_ids(jax.random.fold_in(key_of[4], 71), 0),
    }


def fourier_table(orders, pixels, length):
    phases = (orders[:, None] * pixels[None, :]) % length
    angles = phases.astype(jnp.float32) * (2.0 * jnp.pi / length)
    factor = length ** -0.5
    cos_table = (jnp.cos(angles) * factor).astype(jnp.bfloat16)
    sin_table = (jnp.sin(angles) * factor).astype(jnp.bfloat16)
    return cos_table, sin_table


def reference(sky_map, legendre, conv_weight, block_ids):
    orders = (block_ids[:, None] * MBLK + jnp.arange(MBLK, dtype=jnp.int32)[None, :]).reshape(-1).astype(jnp.int32)
    pixels = jnp.arange(NPHI, dtype=jnp.int32)
    cos_table, sin_table = fourier_table(orders, pixels, NPHI)
    flat_rows = sky_map.reshape(CYCLES * C, NPHI)
    contract = (((1,), (1,)), ((), ()))
    real_part = lax.dot_general(cos_table, flat_rows, contract, preferred_element_type=jnp.float32)
    imag_part = -lax.dot_general(sin_table, flat_rows, contract, preferred_element_type=jnp.float32)
    fourier = jnp.stack([real_part, imag_part], axis=1).reshape(M, 2, CYCLES, C)
    spectra = jnp.transpose(fourier, (2, 1, 3, 0)).reshape(CYCLES, 2 * C, M).astype(jnp.bfloat16)
    band_tiles = legendre.reshape(N_LAT, R_DEV, L, M)
    band_spectra = spectra.reshape(N_LAT, R_DEV, 2 * C, M)

    def add_band(running, pair):
        tile_rows, spectra_rows = pair
        term = jnp.einsum("rlm,rkm->lkm", tile_rows.astype(jnp.float32), spectra_rows.astype(jnp.float32))
        return running + term, None

    total, _ = lax.scan(add_band, jnp.zeros((L, 2 * C, M), jnp.float32), (band_tiles, band_spectra))
    degree_ids = jnp.arange(L, dtype=jnp.int32)
    harmonics = jnp.where(degree_ids[:, None, None] >= orders[None, None, :], total, jnp.float32(0.0))
    padded = jnp.concatenate([sky_map[:, :, NPHI - KW:], sky_map, sky_map[:, :, :KW]], axis=2)
    pixel_sum = jnp.zeros((CYCLES, C, NPHI), jnp.float32)
    for offset in range(2 * KW + 1):
        pixel_sum = pixel_sum + jnp.einsum("oc,rcp->rop", conv_weight[offset].astype(jnp.float32), padded[:, :, offset:offset + NPHI].astype(jnp.float32))
    local_conv = pixel_sum.astype(jnp.bfloat16)
    return harmonics, local_conv
```

```python
import functools

import jax
import jax.numpy as jnp
from jax import lax
from jax.experimental import pallas as pl
from jax.experimental.pallas import tpu as pltpu
from jax.sharding import PartitionSpec as P

TILE = 16


def rotated(shard, axis, by):
    peers = lax.axis_size(axis)
    return lax.ppermute(shard, axis, [(i, (i + by) % peers) for i in range(peers)])


def padded_cycle(block, width):
    low = rotated(block[:, :, -width:], "lon", 1)
    high = rotated(block[:, :, :width], "lon", -1)
    return jnp.concatenate([low, block, high], axis=2)


def angle_pair(phases, length):
    angles = phases.astype(jnp.float32) * (2.0 * jnp.pi / length)
    return jnp.cos(angles), jnp.sin(angles)


def fourier_tables(orders, first_pixel, segment, length):
    fine = 128
    coarse_pixels = first_pixel + fine * jnp.arange(segment // fine, dtype=jnp.int32)
    fine_pixels = jnp.arange(fine, dtype=jnp.int32)
    cos_a, sin_a = angle_pair((orders[:, None] * coarse_pixels[None, :]) % length, length)
    cos_b, sin_b = angle_pair((orders[:, None] * fine_pixels[None, :]) % length, length)
    factor = length ** (-0.5)
    cos_a, sin_a = (cos_a * factor)[:, :, None], (sin_a * factor)[:, :, None]
    cos_b, sin_b = cos_b[:, None, :], sin_b[:, None, :]
    cos_table = (cos_a * cos_b - sin_a * sin_b).astype(jnp.bfloat16)
    sin_table = (sin_a * cos_b + cos_a * sin_b).astype(jnp.bfloat16)
    shape = (orders.shape[0], segment)
    return cos_table.reshape(shape), sin_table.reshape(shape)


def band_kernel(slab_ref, leg_ref, spec_ref, out_ref):
    del slab_ref
    rows, parts = spec_ref.shape[0], spec_ref.shape[1]

    @pl.loop(0, leg_ref.shape[1] // TILE)
    def _(tile):
        span = pl.ds(pl.multiple_of(tile * TILE, TILE), TILE)
        sums = [None] * parts
        for r in range(rows):
            leg = leg_ref[r, span, :].astype(jnp.float32).reshape(TILE // 8, 8, -1)
            for k in range(parts):
                term = leg * spec_ref[r, k][None]
                sums[k] = term if sums[k] is None else sums[k] + term
        for k in range(parts):
            out_ref[k, span, :] = sums[k].reshape(TILE, -1).astype(out_ref.dtype)


def band_partial(legendre, spec_rows, slab, share, kind):
    rows, _, width = legendre.shape
    parts = spec_rows.shape[1]
    step = min(share, 64)
    steps = share // step
    return pl.pallas_call(
        band_kernel,
        out_shape=jax.ShapeDtypeStruct((parts, share, width), kind),
        grid_spec=pltpu.PrefetchScalarGridSpec(
            num_scalar_prefetch=1,
            grid=(steps,),
            in_specs=[
                pl.BlockSpec((rows, step, width), lambda i, s: (0, s[0] * steps + i, 0)),
                pl.BlockSpec((rows, parts, 8, width), lambda i, s: (0, 0, 0, 0)),
            ],
            out_specs=pl.BlockSpec((parts, step, width), lambda i, s: (0, i, 0)),
        ),
        cost_estimate=pl.CostEstimate(
            flops=2 * rows * parts * share * width,
            bytes_accessed=16 * 2 * rows * share * width,
            transcendentals=0,
        ),
    )(slab.reshape(1), legendre, spec_rows)


def chain_tables(n):
    order, up, down = [], [], []
    for z in range(n):
        need = [(n - 1, 2, z)]
        need += [(n - 1 + z - d, 0, d) for d in range(z + 1, n)]
        need += [(n - 1 - z + d, 1, d) for d in range(z)]
        order.append([d for _, _, d in sorted(need)])
    for t in range(n - 1):
        up.append([order[z].index(n - 1 - t + z) if z <= t else None for z in range(n)])
        down.append([order[z].index(t - n + 1 + z) if n - 1 - z <= t else None for z in range(n)])
    return order, up, down


def chosen(chunks, table, z):
    picks = sorted({e for e in table if e is not None})
    value = chunks[picks[0]]
    for e in picks[1:]:
        here = functools.reduce(jnp.logical_or, [z == i for i, p in enumerate(table) if p == e])
        value = jnp.where(here, chunks[e], value)
    return value


def on_device(sky_map, legendre, conv_weight, block_ids):
    cycles_dev, channels, segment = sky_map.shape
    lat_count, lon_count = lax.axis_size("lat"), lax.axis_size("lon")
    lat_index, lon_index = lax.axis_index("lat"), lax.axis_index("lon")
    degrees, block_size = legendre.shape[1:]
    length = segment * lon_count
    orders = (
        block_ids[:, None] * block_size + jnp.arange(block_size, dtype=jnp.int32)[None, :]
    ).reshape(-1)
    width = conv_weight.shape[0] // 2

    flat_rows = sky_map.reshape(cycles_dev * channels, segment)
    cos_table, sin_table = fourier_tables(orders, lon_index * segment, segment, length)
    contract = (((1,), (1,)), ((), ()))
    real_part = lax.dot_general(flat_rows, cos_table, contract, preferred_element_type=jnp.float32)
    imag_part = -lax.dot_general(flat_rows, sin_table, contract, preferred_element_type=jnp.float32)

    def m_block(owner):
        return jnp.stack(
            [
                lax.dynamic_slice_in_dim(part, owner * block_size, block_size, 1)
                for part in (real_part, imag_part)
            ]
        )

    sums = m_block(lon_index)
    arrived = [
        rotated(m_block((lon_index + by) % lon_count).astype(jnp.bfloat16), "lon", by)
        for by in range(1, lon_count)
    ]
    for block in arrived:
        sums = sums + block.astype(jnp.float32)
    spectra = sums.astype(jnp.bfloat16).reshape(2, cycles_dev, channels, block_size)
    spectra = jnp.transpose(spectra, (1, 0, 2, 3)).reshape(cycles_dev, 2 * channels, 1, block_size)
    spec_rows = jnp.broadcast_to(
        spectra.astype(jnp.float32), (cycles_dev, 2 * channels, 8, block_size)
    )

    share = degrees // lat_count
    n = lat_count // 2
    z, x = lat_index // 2, lat_index % 2
    order, up_table, down_table = chain_tables(n)
    order_of = jnp.array(order, jnp.int32)[z]
    pair_swap = [(i, i ^ 1) for i in range(lat_count)]
    given = [
        lax.ppermute(
            band_partial(legendre, spec_rows, order_of[e] * 2 + 1 - x, share, jnp.bfloat16),
            "lat",
            pair_swap,
        )
        for e in range(n)
    ]
    chunks = [
        band_partial(legendre, spec_rows, order_of[e] * 2 + x, share, jnp.float32)
        + given[e].astype(jnp.float32)
        for e in range(n)
    ]
    from_low = from_high = None
    for t in range(n - 1):
        up, down = chosen(chunks, up_table[t], z), chosen(chunks, down_table[t], z)
        if t:
            up = up + from_low.astype(jnp.float32)
            down = down + from_high.astype(jnp.float32)
        up_pairs = [(2 * i + j, 2 * i + 2 + j) for i in range(t + 1) for j in range(2)]
        down_pairs = [(2 * i + j, 2 * i - 2 + j) for i in range(n - 1 - t, n) for j in range(2)]
        from_low = lax.ppermute(up.astype(jnp.bfloat16), "lat", up_pairs)
        from_high = lax.ppermute(down.astype(jnp.bfloat16), "lat", down_pairs)
    summed = chunks[n - 1]
    if n > 1:
        summed = summed + from_low.astype(jnp.float32) + from_high.astype(jnp.float32)
    summed = jnp.transpose(summed, (1, 0, 2))
    degree_ids = lat_index * share + jnp.arange(share, dtype=jnp.int32)
    own_orders = lax.dynamic_slice_in_dim(orders, lon_index * block_size, block_size, 0)
    harmonics = jnp.where(
        degree_ids[:, None, None] >= own_orders[None, None, :], summed, jnp.float32(0.0)
    )

    padded = padded_cycle(sky_map, width)
    pixel_sum = jnp.zeros((cycles_dev, channels, segment), jnp.float32)
    for offset in range(2 * width + 1):
        pixel_sum = pixel_sum + jnp.einsum(
            "oc,rcp->rop",
            conv_weight[offset],
            padded[:, :, offset : offset + segment],
            preferred_element_type=jnp.float32,
        )
    return harmonics, pixel_sum.astype(jnp.bfloat16)


def solution(mesh):
    return jax.shard_map(
        on_device,
        mesh=mesh,
        in_specs=(P("lat", None, "lon"), P("lat", None, "lon"), P(), P()),
        out_specs=(P("lat", None, "lon"), P("lat", None, "lon")),
        check_vma=False,
    )
```

```python
import functools

import jax
import jax.numpy as jnp
from jax import lax
from jax.experimental import pallas as pl
from jax.experimental.pallas import tpu as pltpu
from jax.sharding import PartitionSpec as P

TILE = 16


def rotated(shard, axis, by):
    peers = lax.axis_size(axis)
    return lax.ppermute(shard, axis, [(i, (i + by) % peers) for i in range(peers)])


def padded_cycle(block, width):
    low = rotated(block[:, :, -width:], "lon", 1)
    high = rotated(block[:, :, :width], "lon", -1)
    return jnp.concatenate([low, block, high], axis=2)


def angle_pair(phases, length):
    angles = phases.astype(jnp.float32) * (2.0 * jnp.pi / length)
    return jnp.cos(angles), jnp.sin(angles)


def fourier_tables(orders, first_pixel, segment, length):
    fine = 128
    coarse_pixels = first_pixel + fine * jnp.arange(segment // fine, dtype=jnp.int32)
    fine_pixels = jnp.arange(fine, dtype=jnp.int32)
    cos_a, sin_a = angle_pair((orders[:, None] * coarse_pixels[None, :]) % length, length)
    cos_b, sin_b = angle_pair((orders[:, None] * fine_pixels[None, :]) % length, length)
    factor = length ** (-0.5)
    cos_a, sin_a = (cos_a * factor)[:, :, None], (sin_a * factor)[:, :, None]
    cos_b, sin_b = cos_b[:, None, :], sin_b[:, None, :]
    cos_table = (cos_a * cos_b - sin_a * sin_b).astype(jnp.bfloat16)
    sin_table = (sin_a * cos_b + cos_a * sin_b).astype(jnp.bfloat16)
    shape = (orders.shape[0], segment)
    return cos_table.reshape(shape), sin_table.reshape(shape)


def chunk_at(e, z, n):
    low, high = jnp.minimum(z, n - 1 - z), jnp.maximum(z, n - 1 - z)
    single = e < high - low
    late = e - (high - low)
    step = jnp.where(single, low + e, high + late // 2)
    upward = jnp.where(single, 2 * z < n - 1, late % 2 == 0)
    return jnp.where(upward, n - 1 - step + z, step - (n - 1) + z)


def lat_kernel(
    n, piece, leg_ref, spec_ref, out_ref,
    leg_buf, give, got, own, up_out, up_in, down_out, down_in,
    leg_sem, give_sem, got_sem, up_send, up_recv, down_send, down_recv,
):
    lat = lax.axis_index("lat")
    z, x = lat // 2, lat % 2
    rows, parts = spec_ref.shape[0], spec_ref.shape[1]
    split = give.shape[0] // n
    share = piece * split
    total = n * split

    barrier = pltpu.get_barrier_semaphore()

    def greet(device):
        pl.semaphore_signal(barrier, inc=1, device_id={"lat": device})

    greet(z * 2 + 1 - x)

    @pl.when(z > 0)
    def _():
        greet(lat - 2)

    @pl.when(z < n - 1)
    def _():
        greet(lat + 2)

    def load(i, kind, slot):
        slab = chunk_at(i // split, z, n) * 2 + (1 - x if kind == 0 else x)
        first = pl.multiple_of(slab * share + (i % split) * piece, piece)
        return pltpu.make_async_copy(
            leg_ref.at[:, pl.ds(first, piece), :], leg_buf.at[kind, slot], leg_sem.at[kind, slot]
        )

    load(0, 0, 0).start()
    load(0, 1, 0).start()
    pl.semaphore_wait(barrier, 1 + jnp.minimum(z, 1) + jnp.minimum(n - 1 - z, 1))

    def remote(source, target, send, recv, index, device):
        return pltpu.make_async_remote_copy(
            src_ref=source.at[index],
            dst_ref=target.at[index],
            send_sem=send.at[index],
            recv_sem=recv.at[index],
            device_id={"lat": device},
        )

    def pair_copy(i):
        return remote(give, got, give_sem, got_sem, i, z * 2 + 1 - x)

    def up_copy(i):
        return remote(up_out, up_in, up_send, up_recv, i, jnp.minimum(lat + 2, 2 * n - 2 + x))

    def down_copy(i):
        return remote(down_out, down_in, down_send, down_recv, i, jnp.maximum(lat - 2, x))

    def contract(kind, slot, target, i):
        @pl.loop(0, piece // TILE)
        def _(tile):
            span = pl.ds(pl.multiple_of(tile * TILE, TILE), TILE)
            sums = [None] * parts
            for r in range(rows):
                leg = leg_buf[kind, slot, r, span, :].astype(jnp.float32)
                leg = leg.reshape(TILE // 8, 8, -1)
                for k in range(parts):
                    term = leg * spec_ref[r, k][None]
                    sums[k] = term if sums[k] is None else sums[k] + term
            for k in range(parts):
                target[i, k, span, :] = sums[k].reshape(TILE, -1).astype(target.dtype)

    def forward(t, h, e, arrives, copy, outbox, inbox):
        here, before = t * split + h, (t - 1) * split + h

        @pl.when(arrives)
        def _():
            copy(before).wait_recv()

            @pl.loop(0, parts)
            def _(k):
                value = own[e * split + h, k] + inbox[before, k].astype(jnp.float32)
                outbox[here, k] = value.astype(outbox.dtype)

        @pl.when(jnp.logical_not(arrives))
        def _():
            @pl.loop(0, parts)
            def _(k):
                outbox[here, k] = own[e * split + h, k].astype(outbox.dtype)

        copy(here).start()

    def settle(i):
        t, h = i // split, i % split
        pair_copy(i).wait_recv()

        @pl.loop(0, parts)
        def _(k):
            own[i, k] = own[i, k] + got[i, k].astype(jnp.float32)

        ups, downs = t - z, t - (n - 1 - z)

        @pl.when((t < n - 1) & (ups >= 0))
        def _():
            e = ups + jnp.maximum(downs, 0)
            forward(t, h, e, (z > 0), up_copy, up_out, up_in)

        @pl.when((t < n - 1) & (downs >= 0))
        def _():
            e = downs + jnp.maximum(ups + 1, 0)
            forward(t, h, e, (z < n - 1), down_copy, down_out, down_in)

    @pl.loop(0, total)
    def _(i):
        slot = i % 2

        @pl.when(i + 1 < total)
        def _():
            load(i + 1, 0, 1 - slot).start()
            load(i + 1, 1, 1 - slot).start()

        load(i, 0, slot).wait()
        contract(0, slot, give, i)
        pair_copy(i).start()
        load(i, 1, slot).wait()
        contract(1, slot, own, i)

        @pl.when(i > 0)
        def _():
            settle(i - 1)

    settle(total - 1)

    for h in range(split):
        last, here = (n - 2) * split + h, (n - 1) * split + h
        rows_out = pl.ds(h * piece, piece)

        @pl.when(z > 0)
        def _():
            up_copy(last).wait_recv()

            @pl.loop(0, parts)
            def _(k):
                own[here, k] = own[here, k] + up_in[last, k].astype(jnp.float32)

        @pl.when(z < n - 1)
        def _():
            down_copy(last).wait_recv()

            @pl.loop(0, parts)
            def _(k):
                own[here, k] = own[here, k] + down_in[last, k].astype(jnp.float32)

        @pl.loop(0, parts)
        def _(k):
            out_ref[k, rows_out, :] = own[here, k]

    @pl.loop(0, total)
    def _(i):
        pair_copy(i).wait_send()

    @pl.loop(0, (n - 1) * split)
    def _(i):
        @pl.when(z <= i // split)
        def _():
            up_copy(i).wait_send()

        @pl.when(n - 1 - z <= i // split)
        def _():
            down_copy(i).wait_send()


def lat_sums(legendre, spec_rows, share, n):
    rows, _, width = legendre.shape
    parts = spec_rows.shape[1]
    piece = min(share, 64)
    split = share // piece
    total, links = n * split, (n - 1) * split
    block = (parts, piece, width)
    wire = jnp.bfloat16
    return pl.pallas_call(
        functools.partial(lat_kernel, n, piece),
        out_shape=jax.ShapeDtypeStruct((parts, share, width), jnp.float32),
        in_specs=[
            pl.BlockSpec(memory_space=pl.ANY),
            pl.BlockSpec(memory_space=pltpu.VMEM),
        ],
        out_specs=pl.BlockSpec(memory_space=pltpu.VMEM),
        scratch_shapes=[
            pltpu.VMEM((2, 2, rows, piece, width), legendre.dtype),
            pltpu.VMEM((total, *block), wire),
            pltpu.VMEM((total, *block), wire),
            pltpu.VMEM((total, *block), jnp.float32),
            pltpu.VMEM((links, *block), wire),
            pltpu.VMEM((links, *block), wire),
            pltpu.VMEM((links, *block), wire),
            pltpu.VMEM((links, *block), wire),
            pltpu.SemaphoreType.DMA((2, 2)),
            pltpu.SemaphoreType.DMA((total,)),
            pltpu.SemaphoreType.DMA((total,)),
            pltpu.SemaphoreType.DMA((links,)),
            pltpu.SemaphoreType.DMA((links,)),
            pltpu.SemaphoreType.DMA((links,)),
            pltpu.SemaphoreType.DMA((links,)),
        ],
        compiler_params=pltpu.CompilerParams(
            collective_id=0, has_side_effects=True, vmem_limit_bytes=52 * 2**20
        ),
        cost_estimate=pl.CostEstimate(
            flops=10**10, bytes_accessed=legendre.size * 2, transcendentals=0
        ),
    )(legendre, spec_rows)


def on_device(sky_map, legendre, conv_weight, block_ids):
    cycles_dev, channels, segment = sky_map.shape
    lat_count, lon_count = lax.axis_size("lat"), lax.axis_size("lon")
    lat_index, lon_index = lax.axis_index("lat"), lax.axis_index("lon")
    degrees, block_size = legendre.shape[1:]
    length = segment * lon_count
    orders = (
        block_ids[:, None] * block_size + jnp.arange(block_size, dtype=jnp.int32)[None, :]
    ).reshape(-1)
    width = conv_weight.shape[0] // 2

    flat_rows = sky_map.reshape(cycles_dev * channels, segment)
    cos_table, sin_table = fourier_tables(orders, lon_index * segment, segment, length)
    contract = (((1,), (1,)), ((), ()))
    real_part = lax.dot_general(flat_rows, cos_table, contract, preferred_element_type=jnp.float32)
    imag_part = -lax.dot_general(flat_rows, sin_table, contract, preferred_element_type=jnp.float32)

    def m_block(owner):
        return jnp.stack(
            [
                lax.dynamic_slice_in_dim(part, owner * block_size, block_size, 1)
                for part in (real_part, imag_part)
            ]
        )

    sums = m_block(lon_index)
    arrived = [
        rotated(m_block((lon_index + by) % lon_count).astype(jnp.bfloat16), "lon", by)
        for by in range(1, lon_count)
    ]
    for block in arrived:
        sums = sums + block.astype(jnp.float32)
    spectra = sums.astype(jnp.bfloat16).reshape(2, cycles_dev, channels, block_size)
    spectra = jnp.transpose(spectra, (1, 0, 2, 3)).reshape(cycles_dev, 2 * channels, 1, block_size)
    spec_rows = jnp.broadcast_to(
        spectra.astype(jnp.float32), (cycles_dev, 2 * channels, 8, block_size)
    )

    share = degrees // lat_count
    summed = lat_sums(legendre, spec_rows, share, lat_count // 2)
    summed = jnp.transpose(summed, (1, 0, 2))
    degree_ids = lat_index * share + jnp.arange(share, dtype=jnp.int32)
    own_orders = lax.dynamic_slice_in_dim(orders, lon_index * block_size, block_size, 0)
    harmonics = jnp.where(
        degree_ids[:, None, None] >= own_orders[None, None, :], summed, jnp.float32(0.0)
    )

    padded = padded_cycle(sky_map, width)
    pixel_sum = jnp.zeros((cycles_dev, channels, segment), jnp.float32)
    for offset in range(2 * width + 1):
        pixel_sum = pixel_sum + jnp.einsum(
            "oc,rcp->rop",
            conv_weight[offset],
            padded[:, :, offset : offset + segment],
            preferred_element_type=jnp.float32,
        )
    return harmonics, pixel_sum.astype(jnp.bfloat16)


def solution(mesh):
    return jax.shard_map(
        on_device,
        mesh=mesh,
        in_specs=(P("lat", None, "lon"), P("lat", None, "lon"), P(), P()),
        out_specs=(P("lat", None, "lon"), P("lat", None, "lon")),
        check_vma=False,
    )
```

```python
import functools

import jax
import jax.numpy as jnp
from jax import lax
from jax.experimental import pallas as pl
from jax.experimental.pallas import tpu as pltpu
from jax.sharding import PartitionSpec as P

TILE = 16


def rotated(shard, axis, by):
    peers = lax.axis_size(axis)
    return lax.ppermute(shard, axis, [(i, (i + by) % peers) for i in range(peers)])


def padded_cycle(block, width):
    low = rotated(block[:, :, -width:], "lon", 1)
    high = rotated(block[:, :, :width], "lon", -1)
    fill = jnp.zeros(block.shape[:2] + (128 - 2 * width,), block.dtype)
    return jnp.concatenate([low, block, high, fill], axis=2)


def angle_pair(phases, length):
    angles = phases.astype(jnp.float32) * (2.0 * jnp.pi / length)
    return jnp.cos(angles), jnp.sin(angles)


def fourier_tables(orders, first_pixel, segment, length):
    fine = 128
    coarse_pixels = first_pixel + fine * jnp.arange(segment // fine, dtype=jnp.int32)
    fine_pixels = jnp.arange(fine, dtype=jnp.int32)
    cos_a, sin_a = angle_pair((orders[:, None] * coarse_pixels[None, :]) % length, length)
    cos_b, sin_b = angle_pair((orders[:, None] * fine_pixels[None, :]) % length, length)
    factor = length ** (-0.5)
    cos_a, sin_a = (cos_a * factor)[:, :, None], (sin_a * factor)[:, :, None]
    cos_b, sin_b = cos_b[:, None, :], sin_b[:, None, :]
    cos_table = (cos_a * cos_b - sin_a * sin_b).astype(jnp.bfloat16)
    sin_table = (sin_a * cos_b + cos_a * sin_b).astype(jnp.bfloat16)
    shape = (orders.shape[0], segment)
    return cos_table.reshape(shape), sin_table.reshape(shape)


def chunk_at(e, z, n):
    low, high = jnp.minimum(z, n - 1 - z), jnp.maximum(z, n - 1 - z)
    single = e < high - low
    late = e - (high - low)
    step = jnp.where(single, low + e, high + late // 2)
    upward = jnp.where(single, 2 * z < n - 1, late % 2 == 0)
    return jnp.where(upward, n - 1 - step + z, step - (n - 1) + z)


def lat_kernel(
    n, piece, leg_ref, spec_ref, weight_ref, padded_ref, out_ref, conv_ref,
    leg_buf, give, got, own, up_out, up_in, down_out, down_in,
    leg_sem, give_sem, got_sem, up_send, up_recv, down_send, down_recv,
):
    lat = lax.axis_index("lat")
    z, x = lat // 2, lat % 2
    rows, parts = spec_ref.shape[0], spec_ref.shape[1]
    split = give.shape[0] // n
    share = piece * split
    total = n * split

    barrier = pltpu.get_barrier_semaphore()

    def greet(device):
        pl.semaphore_signal(barrier, inc=1, device_id={"lat": device})

    greet(z * 2 + 1 - x)

    @pl.when(z > 0)
    def _():
        greet(lat - 2)

    @pl.when(z < n - 1)
    def _():
        greet(lat + 2)

    def load(i, kind, slot):
        slab = chunk_at(i // split, z, n) * 2 + (1 - x if kind == 0 else x)
        first = pl.multiple_of(slab * share + (i % split) * piece, piece)
        return pltpu.make_async_copy(
            leg_ref.at[:, pl.ds(first, piece), :], leg_buf.at[kind, slot], leg_sem.at[kind, slot]
        )

    load(0, 0, 0).start()
    load(0, 1, 0).start()
    pl.semaphore_wait(barrier, 1 + jnp.minimum(z, 1) + jnp.minimum(n - 1 - z, 1))

    def remote(source, target, send, recv, index, device):
        return pltpu.make_async_remote_copy(
            src_ref=source.at[index],
            dst_ref=target.at[index],
            send_sem=send.at[index],
            recv_sem=recv.at[index],
            device_id={"lat": device},
        )

    def pair_copy(i):
        return remote(give, got, give_sem, got_sem, i, z * 2 + 1 - x)

    def up_copy(i):
        return remote(up_out, up_in, up_send, up_recv, i, jnp.minimum(lat + 2, 2 * n - 2 + x))

    def down_copy(i):
        return remote(down_out, down_in, down_send, down_recv, i, jnp.maximum(lat - 2, x))

    def contract(kind, slot, target, i):
        @pl.loop(0, piece // TILE)
        def _(tile):
            span = pl.ds(pl.multiple_of(tile * TILE, TILE), TILE)
            sums = [None] * parts
            for r in range(rows):
                leg = leg_buf[kind, slot, r, span, :].astype(jnp.float32)
                leg = leg.reshape(TILE // 8, 8, -1)
                for k in range(parts):
                    term = leg * spec_ref[r, k][None]
                    sums[k] = term if sums[k] is None else sums[k] + term
            for k in range(parts):
                target[i, k, span, :] = sums[k].reshape(TILE, -1).astype(target.dtype)

    cycles, _, segment = conv_ref.shape
    batch = -(-cycles // total)
    taps = weight_ref.shape[1] // padded_ref.shape[1]

    def convolve(r):
        row = padded_ref[r].astype(jnp.float32)
        wide = row.shape[1]
        shifted = [row] + [pltpu.roll(row, wide - t, 1) for t in range(1, taps)]
        windows = jnp.concatenate([w[:, :segment] for w in shifted], axis=0)
        conv_ref[r] = jnp.dot(
            weight_ref[...], windows.astype(jnp.bfloat16), preferred_element_type=jnp.float32
        ).astype(conv_ref.dtype)

    def forward(t, h, e, arrives, copy, outbox, inbox):
        here, before = t * split + h, (t - 1) * split + h

        @pl.when(arrives)
        def _():
            copy(before).wait_recv()

            @pl.loop(0, parts)
            def _(k):
                value = own[e * split + h, k] + inbox[before, k].astype(jnp.float32)
                outbox[here, k] = value.astype(outbox.dtype)

        @pl.when(jnp.logical_not(arrives))
        def _():
            @pl.loop(0, parts)
            def _(k):
                outbox[here, k] = own[e * split + h, k].astype(outbox.dtype)

        copy(here).start()

    def settle(i):
        t, h = i // split, i % split
        pair_copy(i).wait_recv()

        @pl.loop(0, parts)
        def _(k):
            own[i, k] = own[i, k] + got[i, k].astype(jnp.float32)

        ups, downs = t - z, t - (n - 1 - z)

        @pl.when((t < n - 1) & (ups >= 0))
        def _():
            e = ups + jnp.maximum(downs, 0)
            forward(t, h, e, (z > 0), up_copy, up_out, up_in)

        @pl.when((t < n - 1) & (downs >= 0))
        def _():
            e = downs + jnp.maximum(ups + 1, 0)
            forward(t, h, e, (z < n - 1), down_copy, down_out, down_in)

    @pl.loop(0, total)
    def _(i):
        slot = i % 2

        @pl.when(i + 1 < total)
        def _():
            load(i + 1, 0, 1 - slot).start()
            load(i + 1, 1, 1 - slot).start()

        load(i, 0, slot).wait()
        contract(0, slot, give, i)
        pair_copy(i).start()
        load(i, 1, slot).wait()
        contract(1, slot, own, i)

        @pl.loop(0, batch)
        def _(j):
            @pl.when(i * batch + j < cycles)
            def _():
                convolve(jnp.minimum(i * batch + j, cycles - 1))

        @pl.when(i > 0)
        def _():
            settle(i - 1)

    settle(total - 1)

    for h in range(split):
        last, here = (n - 2) * split + h, (n - 1) * split + h
        rows_out = pl.ds(h * piece, piece)

        @pl.when(z > 0)
        def _():
            up_copy(last).wait_recv()

            @pl.loop(0, parts)
            def _(k):
                own[here, k] = own[here, k] + up_in[last, k].astype(jnp.float32)

        @pl.when(z < n - 1)
        def _():
            down_copy(last).wait_recv()

            @pl.loop(0, parts)
            def _(k):
                own[here, k] = own[here, k] + down_in[last, k].astype(jnp.float32)

        @pl.loop(0, parts)
        def _(k):
            out_ref[k, rows_out, :] = own[here, k]

    @pl.loop(0, total)
    def _(i):
        pair_copy(i).wait_send()

    @pl.loop(0, (n - 1) * split)
    def _(i):
        @pl.when(z <= i // split)
        def _():
            up_copy(i).wait_send()

        @pl.when(n - 1 - z <= i // split)
        def _():
            down_copy(i).wait_send()


def lat_sums(legendre, spec_rows, weights, padded, conv_shape, share, n):
    rows, _, width = legendre.shape
    parts = spec_rows.shape[1]
    piece = min(share, 64)
    split = share // piece
    total, links = n * split, (n - 1) * split
    block = (parts, piece, width)
    wire = jnp.bfloat16
    return pl.pallas_call(
        functools.partial(lat_kernel, n, piece),
        out_shape=(
            jax.ShapeDtypeStruct((parts, share, width), jnp.float32),
            jax.ShapeDtypeStruct(conv_shape, jnp.bfloat16),
        ),
        in_specs=[pl.BlockSpec(memory_space=pl.ANY)]
        + [pl.BlockSpec(memory_space=pltpu.VMEM)] * 3,
        out_specs=[pl.BlockSpec(memory_space=pltpu.VMEM)] * 2,
        scratch_shapes=[
            pltpu.VMEM((2, 2, rows, piece, width), legendre.dtype),
            pltpu.VMEM((total, *block), wire),
            pltpu.VMEM((total, *block), wire),
            pltpu.VMEM((total, *block), jnp.float32),
            pltpu.VMEM((links, *block), wire),
            pltpu.VMEM((links, *block), wire),
            pltpu.VMEM((links, *block), wire),
            pltpu.VMEM((links, *block), wire),
            pltpu.SemaphoreType.DMA((2, 2)),
            pltpu.SemaphoreType.DMA((total,)),
            pltpu.SemaphoreType.DMA((total,)),
            pltpu.SemaphoreType.DMA((links,)),
            pltpu.SemaphoreType.DMA((links,)),
            pltpu.SemaphoreType.DMA((links,)),
            pltpu.SemaphoreType.DMA((links,)),
        ],
        compiler_params=pltpu.CompilerParams(
            collective_id=0, has_side_effects=True, vmem_limit_bytes=52 * 2**20
        ),
        cost_estimate=pl.CostEstimate(
            flops=10**10, bytes_accessed=legendre.size * 2, transcendentals=0
        ),
    )(legendre, spec_rows, weights, padded)


def on_device(sky_map, legendre, conv_weight, block_ids):
    cycles_dev, channels, segment = sky_map.shape
    lat_count, lon_count = lax.axis_size("lat"), lax.axis_size("lon")
    lat_index, lon_index = lax.axis_index("lat"), lax.axis_index("lon")
    degrees, block_size = legendre.shape[1:]
    length = segment * lon_count
    orders = (
        block_ids[:, None] * block_size + jnp.arange(block_size, dtype=jnp.int32)[None, :]
    ).reshape(-1)
    width = conv_weight.shape[0] // 2

    flat_rows = sky_map.reshape(cycles_dev * channels, segment)
    cos_table, sin_table = fourier_tables(orders, lon_index * segment, segment, length)
    contract = (((1,), (1,)), ((), ()))
    real_part = lax.dot_general(flat_rows, cos_table, contract, preferred_element_type=jnp.float32)
    imag_part = -lax.dot_general(flat_rows, sin_table, contract, preferred_element_type=jnp.float32)

    def m_block(owner):
        return jnp.stack(
            [
                lax.dynamic_slice_in_dim(part, owner * block_size, block_size, 1)
                for part in (real_part, imag_part)
            ]
        )

    sums = m_block(lon_index)
    arrived = [
        rotated(m_block((lon_index + by) % lon_count).astype(jnp.bfloat16), "lon", by)
        for by in range(1, lon_count)
    ]
    for block in arrived:
        sums = sums + block.astype(jnp.float32)
    spectra = sums.astype(jnp.bfloat16).reshape(2, cycles_dev, channels, block_size)
    spectra = jnp.transpose(spectra, (1, 0, 2, 3)).reshape(cycles_dev, 2 * channels, 1, block_size)
    spec_rows = jnp.broadcast_to(
        spectra.astype(jnp.float32), (cycles_dev, 2 * channels, 8, block_size)
    )

    share = degrees // lat_count
    padded = padded_cycle(sky_map, width)
    weights = jnp.transpose(conv_weight, (1, 0, 2)).reshape(channels, -1)
    summed, local_conv = lat_sums(
        legendre, spec_rows, weights, padded, sky_map.shape, share, lat_count // 2
    )
    summed = jnp.transpose(summed, (1, 0, 2))
    degree_ids = lat_index * share + jnp.arange(share, dtype=jnp.int32)
    own_orders = lax.dynamic_slice_in_dim(orders, lon_index * block_size, block_size, 0)
    harmonics = jnp.where(
        degree_ids[:, None, None] >= own_orders[None, None, :], summed, jnp.float32(0.0)
    )
    return harmonics, local_conv


def solution(mesh):
    return jax.shard_map(
        on_device,
        mesh=mesh,
        in_specs=(P("lat", None, "lon"), P("lat", None, "lon"), P(), P()),
        out_specs=(P("lat", None, "lon"), P("lat", None, "lon")),
        check_vma=False,
    )
```

```python
import functools

import jax
import jax.numpy as jnp
from jax import lax
from jax.experimental import pallas as pl
from jax.experimental.pallas import tpu as pltpu
from jax.sharding import PartitionSpec as P

TILE = 16


def rotated(shard, axis, by):
    peers = lax.axis_size(axis)
    return lax.ppermute(shard, axis, [(i, (i + by) % peers) for i in range(peers)])


def padded_cycle(block, width):
    low = rotated(block[:, :, -width:], "lon", 1)
    high = rotated(block[:, :, :width], "lon", -1)
    fill = jnp.zeros(block.shape[:2] + (128 - 2 * width,), block.dtype)
    return jnp.concatenate([low, block, high, fill], axis=2)


def angle_pair(phases, length):
    angles = phases.astype(jnp.float32) * (2.0 * jnp.pi / length)
    return jnp.cos(angles), jnp.sin(angles)


def fourier_tables(orders, first_pixel, segment, length):
    fine = 128
    coarse_pixels = first_pixel + fine * jnp.arange(segment // fine, dtype=jnp.int32)
    fine_pixels = jnp.arange(fine, dtype=jnp.int32)
    cos_a, sin_a = angle_pair((orders[:, None] * coarse_pixels[None, :]) % length, length)
    cos_b, sin_b = angle_pair((orders[:, None] * fine_pixels[None, :]) % length, length)
    factor = length ** (-0.5)
    cos_a, sin_a = (cos_a * factor)[:, :, None], (sin_a * factor)[:, :, None]
    cos_b, sin_b = cos_b[:, None, :], sin_b[:, None, :]
    cos_table = (cos_a * cos_b - sin_a * sin_b).astype(jnp.bfloat16)
    sin_table = (sin_a * cos_b + cos_a * sin_b).astype(jnp.bfloat16)
    shape = (orders.shape[0], segment)
    return cos_table.reshape(shape), sin_table.reshape(shape)


def chunk_at(e, z, n):
    low, high = jnp.minimum(z, n - 1 - z), jnp.maximum(z, n - 1 - z)
    single = e < high - low
    late = e - (high - low)
    step = jnp.where(single, low + e, high + late // 2)
    upward = jnp.where(single, 2 * z < n - 1, late % 2 == 0)
    return jnp.where(upward, n - 1 - step + z, step - (n - 1) + z)


def lat_kernel(
    n, piece, leg_ref, spec_ref, weight_ref, padded_ref, out_ref, conv_ref,
    leg_buf, give, got, own, up_out, up_in, down_out, down_in, relay,
    leg_sem, give_sem, got_sem, up_send, up_recv, down_send, down_recv, hop_send, hop_recv,
):
    lat = lax.axis_index("lat")
    z, x = lat // 2, lat % 2
    rows, parts = spec_ref.shape[0], spec_ref.shape[1]
    split = give.shape[0] // n
    share = piece * split
    total = n * split
    direct = total - split
    degrees, width = leg_ref.shape[1], leg_ref.shape[2]
    lon, half = lax.axis_index("lon"), lax.axis_size("lon") // 2
    lower = lon < half
    across = jnp.where(lower, lon + half, lon - half)

    barrier = pltpu.get_barrier_semaphore()

    def greet(device):
        pl.semaphore_signal(barrier, inc=1, device_id={"lat": device})

    greet(z * 2 + 1 - x)
    pl.semaphore_signal(barrier, inc=1, device_id={"lon": across})

    @pl.when(z > 0)
    def _():
        greet(lat - 2)

    @pl.when(z < n - 1)
    def _():
        greet(lat + 2)

    def load(i, kind, slot):
        slab = chunk_at(i // split, z, n) * 2 + (x if kind == 1 else 1 - x)
        first = pl.multiple_of(slab * share + (i % split) * piece, piece)
        return pltpu.make_async_copy(
            leg_ref.at[:, pl.ds(first, piece), :], leg_buf.at[kind, slot], leg_sem.at[kind, slot]
        )

    load(0, 0, 0).start()
    load(0, 1, 0).start()
    pl.semaphore_wait(barrier, 2 + jnp.minimum(z, 1) + jnp.minimum(n - 1 - z, 1))

    def remote(source, target, send, recv, index, device):
        return pltpu.make_async_remote_copy(
            src_ref=source.at[index],
            dst_ref=target.at[index],
            send_sem=send.at[index],
            recv_sem=recv.at[index],
            device_id={"lat": device},
        )

    def pair_copy(i):
        return remote(give, got, give_sem, got_sem, i, z * 2 + 1 - x)

    def up_copy(i):
        return remote(up_out, up_in, up_send, up_recv, i, jnp.minimum(lat + 2, 2 * n - 2 + x))

    def down_copy(i):
        return remote(down_out, down_in, down_send, down_recv, i, jnp.maximum(lat - 2, x))

    def needed(i, side):
        slab = chunk_at(i // split, z, n) * 2 + side
        top = slab * share + (i % split + 1) * piece
        return (lon < 2 * half - 1) | (top > degrees - width)

    def sent_directly(i):
        return needed(i, 1 - x) & (jnp.logical_not(lower) | (i < direct))

    def hop(number, h):
        source = give.at[direct + h] if number == 0 else relay.at[number - 1, h]
        target = got.at[direct + h] if number == 2 else relay.at[number, h]
        recv = got_sem.at[direct + h] if number == 2 else hop_recv.at[number, h]
        return pltpu.make_async_remote_copy(
            src_ref=source,
            dst_ref=target,
            send_sem=hop_send.at[number, h],
            recv_sem=recv,
            device_id={"lat": z * 2 + 1 - x} if number == 1 else {"lon": across},
        )

    def contract(kind, slot, target, i):
        @pl.loop(0, piece // TILE)
        def _(tile):
            span = pl.ds(pl.multiple_of(tile * TILE, TILE), TILE)
            sums = [None] * parts
            for r in range(rows):
                leg = leg_buf[kind, slot, r, span, :].astype(jnp.float32)
                leg = leg.reshape(TILE // 8, 8, -1)
                for k in range(parts):
                    term = leg * spec_ref[r, k][None]
                    sums[k] = term if sums[k] is None else sums[k] + term
            for k in range(parts):
                target[i, k, span, :] = sums[k].reshape(TILE, -1).astype(target.dtype)

    cycles, _, segment = conv_ref.shape
    batch = -(-cycles // total)
    taps = weight_ref.shape[1] // padded_ref.shape[1]

    def convolve(r):
        row = padded_ref[r].astype(jnp.float32)
        wide = row.shape[1]
        shifted = [row] + [pltpu.roll(row, wide - t, 1) for t in range(1, taps)]
        windows = jnp.concatenate([w[:, :segment] for w in shifted], axis=0)
        conv_ref[r] = jnp.dot(
            weight_ref[...], windows.astype(jnp.bfloat16), preferred_element_type=jnp.float32
        ).astype(conv_ref.dtype)

    def forward(t, h, e, arrives, copy, outbox, inbox):
        here, before = t * split + h, (t - 1) * split + h

        @pl.when(arrives)
        def _():
            copy(before).wait_recv()

            @pl.loop(0, parts)
            def _(k):
                value = own[e * split + h, k] + inbox[before, k].astype(jnp.float32)
                outbox[here, k] = value.astype(outbox.dtype)

        @pl.when(jnp.logical_not(arrives))
        def _():
            @pl.loop(0, parts)
            def _(k):
                outbox[here, k] = own[e * split + h, k].astype(outbox.dtype)

        copy(here).start()

    def settle(i):
        t, h = i // split, i % split

        @pl.when(needed(i, x))
        def _():
            pair_copy(i).wait_recv()

            @pl.loop(0, parts)
            def _(k):
                own[i, k] = own[i, k] + got[i, k].astype(jnp.float32)

        ups, downs = t - z, t - (n - 1 - z)

        @pl.when((t < n - 1) & (ups >= 0))
        def _():
            e = ups + jnp.maximum(downs, 0)
            forward(t, h, e, (z > 0), up_copy, up_out, up_in)

        @pl.when((t < n - 1) & (downs >= 0))
        def _():
            e = downs + jnp.maximum(ups + 1, 0)
            forward(t, h, e, (z < n - 1), down_copy, down_out, down_in)

    @pl.loop(0, total)
    def _(i):
        slot = i % 2

        @pl.when(i + 1 < total)
        def _():
            load(i + 1, 0, 1 - slot).start()
            load(i + 1, 1, 1 - slot).start()

        load(i, 0, slot).wait()

        @pl.when(sent_directly(i))
        def _():
            contract(0, slot, give, i)
            pair_copy(i).start()

        @pl.when(lower & (i < split))
        def _():
            load(direct + i, 2, 1 - slot).start()

        @pl.when(lower & (i >= 1) & (i <= split))
        def _():
            load(direct + i - 1, 2, slot).wait()
            contract(2, slot, give, direct + i - 1)
            hop(0, i - 1).start()

        for number, lag in ((1, 3), (2, 6)):

            @pl.when(jnp.logical_not(lower) & (i >= lag) & (i < lag + split))
            def _():
                hop(number - 1, i - lag).wait_recv()
                hop(number, i - lag).start()

        load(i, 1, slot).wait()
        contract(1, slot, own, i)

        @pl.loop(0, batch)
        def _(j):
            @pl.when(i * batch + j < cycles)
            def _():
                convolve(jnp.minimum(i * batch + j, cycles - 1))

        @pl.when(i > 0)
        def _():
            settle(i - 1)

    settle(total - 1)

    for h in range(split):
        last, here = (n - 2) * split + h, (n - 1) * split + h
        rows_out = pl.ds(h * piece, piece)

        @pl.when(z > 0)
        def _():
            up_copy(last).wait_recv()

            @pl.loop(0, parts)
            def _(k):
                own[here, k] = own[here, k] + up_in[last, k].astype(jnp.float32)

        @pl.when(z < n - 1)
        def _():
            down_copy(last).wait_recv()

            @pl.loop(0, parts)
            def _(k):
                own[here, k] = own[here, k] + down_in[last, k].astype(jnp.float32)

        @pl.loop(0, parts)
        def _(k):
            out_ref[k, rows_out, :] = own[here, k]

    @pl.loop(0, total)
    def _(i):
        @pl.when(sent_directly(i))
        def _():
            pair_copy(i).wait_send()

    @pl.loop(0, split)
    def _(h):
        @pl.when(lower)
        def _():
            hop(0, h).wait_send()

        @pl.when(jnp.logical_not(lower))
        def _():
            hop(1, h).wait_send()
            hop(2, h).wait_send()

    @pl.loop(0, (n - 1) * split)
    def _(i):
        @pl.when(z <= i // split)
        def _():
            up_copy(i).wait_send()

        @pl.when(n - 1 - z <= i // split)
        def _():
            down_copy(i).wait_send()


def lat_sums(legendre, spec_rows, weights, padded, conv_shape, share, n):
    rows, _, width = legendre.shape
    parts = spec_rows.shape[1]
    piece = min(share, 64)
    split = share // piece
    total, links = n * split, (n - 1) * split
    block = (parts, piece, width)
    wire = jnp.bfloat16
    return pl.pallas_call(
        functools.partial(lat_kernel, n, piece),
        out_shape=(
            jax.ShapeDtypeStruct((parts, share, width), jnp.float32),
            jax.ShapeDtypeStruct(conv_shape, jnp.bfloat16),
        ),
        in_specs=[pl.BlockSpec(memory_space=pl.ANY)]
        + [pl.BlockSpec(memory_space=pltpu.VMEM)] * 3,
        out_specs=[pl.BlockSpec(memory_space=pltpu.VMEM)] * 2,
        scratch_shapes=[
            pltpu.VMEM((3, 2, rows, piece, width), legendre.dtype),
            pltpu.VMEM((total, *block), wire),
            pltpu.VMEM((total, *block), wire),
            pltpu.VMEM((total, *block), jnp.float32),
            pltpu.VMEM((links, *block), wire),
            pltpu.VMEM((links, *block), wire),
            pltpu.VMEM((links, *block), wire),
            pltpu.VMEM((links, *block), wire),
            pltpu.VMEM((2, split, *block), wire),
            pltpu.SemaphoreType.DMA((3, 2)),
            pltpu.SemaphoreType.DMA((total,)),
            pltpu.SemaphoreType.DMA((total,)),
            pltpu.SemaphoreType.DMA((links,)),
            pltpu.SemaphoreType.DMA((links,)),
            pltpu.SemaphoreType.DMA((links,)),
            pltpu.SemaphoreType.DMA((links,)),
            pltpu.SemaphoreType.DMA((3, split)),
            pltpu.SemaphoreType.DMA((2, split)),
        ],
        compiler_params=pltpu.CompilerParams(
            collective_id=0, has_side_effects=True, vmem_limit_bytes=52 * 2**20
        ),
        cost_estimate=pl.CostEstimate(
            flops=10**10, bytes_accessed=legendre.size * 2, transcendentals=0
        ),
    )(legendre, spec_rows, weights, padded)


def on_device(sky_map, legendre, conv_weight, block_ids):
    cycles_dev, channels, segment = sky_map.shape
    lat_count, lon_count = lax.axis_size("lat"), lax.axis_size("lon")
    lat_index, lon_index = lax.axis_index("lat"), lax.axis_index("lon")
    degrees, block_size = legendre.shape[1:]
    length = segment * lon_count
    orders = (
        block_ids[:, None] * block_size + jnp.arange(block_size, dtype=jnp.int32)[None, :]
    ).reshape(-1)
    width = conv_weight.shape[0] // 2

    flat_rows = sky_map.reshape(cycles_dev * channels, segment)
    cos_table, sin_table = fourier_tables(orders, lon_index * segment, segment, length)
    contract = (((1,), (1,)), ((), ()))
    real_part = lax.dot_general(flat_rows, cos_table, contract, preferred_element_type=jnp.float32)
    imag_part = -lax.dot_general(flat_rows, sin_table, contract, preferred_element_type=jnp.float32)

    def m_block(owner):
        return jnp.stack(
            [
                lax.dynamic_slice_in_dim(part, owner * block_size, block_size, 1)
                for part in (real_part, imag_part)
            ]
        )

    sums = m_block(lon_index)
    arrived = [
        rotated(m_block((lon_index + by) % lon_count).astype(jnp.bfloat16), "lon", by)
        for by in range(1, lon_count)
    ]
    for block in arrived:
        sums = sums + block.astype(jnp.float32)
    spectra = sums.astype(jnp.bfloat16).reshape(2, cycles_dev, channels, block_size)
    spectra = jnp.transpose(spectra, (1, 0, 2, 3)).reshape(cycles_dev, 2 * channels, 1, block_size)
    spec_rows = jnp.broadcast_to(
        spectra.astype(jnp.float32), (cycles_dev, 2 * channels, 8, block_size)
    )

    share = degrees // lat_count
    padded = padded_cycle(sky_map, width)
    weights = jnp.transpose(conv_weight, (1, 0, 2)).reshape(channels, -1)
    summed, local_conv = lat_sums(
        legendre, spec_rows, weights, padded, sky_map.shape, share, lat_count // 2
    )
    summed = jnp.transpose(summed, (1, 0, 2))
    degree_ids = lat_index * share + jnp.arange(share, dtype=jnp.int32)
    own_orders = lax.dynamic_slice_in_dim(orders, lon_index * block_size, block_size, 0)
    harmonics = jnp.where(
        degree_ids[:, None, None] >= own_orders[None, None, :], summed, jnp.float32(0.0)
    )
    return harmonics, local_conv


def solution(mesh):
    return jax.shard_map(
        on_device,
        mesh=mesh,
        in_specs=(P("lat", None, "lon"), P("lat", None, "lon"), P(), P()),
        out_specs=(P("lat", None, "lon"), P("lat", None, "lon")),
        check_vma=False,
    )
```
